32 devices in a mesh: grp: 2 (over x), seq: 16 (over z, y, core).
Axes of the slice: x: 2, y: 2, z: 4, core: 2. Of those that a mesh axis runs over, the one named last changes fastest.
Arguments:
- queries: bfloat16 [16384, 2048], P(('grp', 'seq')), parts along dimension 0, may hold values from -16 to 16
- key_rows: bfloat16 [16384, 2048], P(('grp', 'seq')), parts along dimension 0, may hold values from -4 to 4
- value_rows: bfloat16 [16384, 2048], P(('grp', 'seq')), parts along dimension 0, may hold values from -6 to 6
- box_bins: int32 [2, 16384], P(None, ('grp', 'seq')), parts along dimension 1, may hold values from 0 to 255
- slopes: float32 [16], replicated, may hold values from 0.05 to 3
- near_lists: int32 [128, 5], P('grp'), parts along dimension 0, may hold values from -1 to 59, as said below
Outputs:
- attended: bfloat16 [16384, 2048], P(('grp', 'seq')), parts along dimension 0
The draws below stay inside these ranges and needn't reach their ends.
There are 2 independent parts, one for each index of `grp`. The reference program is written for one: setup_inputs(seed, part) draws one part's arguments, and reference() takes and returns one part's arrays. A program takes and returns all parts, laid end to end along the dimension named above; an argument that names none is the same for every part. Nothing has to cross between parts.
Inputs may be any that keep to these rules, and one draw needn't show every extreme that they name: `near_lists`: block ids lie on one of the 6 devices before the query block's device, the device of block c being c // 4; the ids listed for one query block differ from one another; the lists of one device's 4 query blocks together name exactly 2 distinct blocks of each of those preceding devices that exist, and -1 stands for the blocks of devices before the first.
All inputs are finite; a program needn't handle non-finite values.
Results may differ from the reference program's by a relative error of at most 0.0038.
Values may be sent and summed in bfloat16 or wider, within the bound.
A program may use at most 128 MiB of HBM per device.

```python
import math
import jax
import jax.numpy as jnp
from jax import lax

H = 16
HD = 128
BLOCK = 128
NEAR = 5
REACH = 6
CAP = 2
GRID = 256
QB = 4
TOKENS = 8192
NBLK = 64


def draw_queries(key, part):
    result = jnp.clip(jax.random.normal(jax.random.fold_in(key, 2), (TOKENS, H * HD), jnp.float32), -4.0, 4.0)
    return result.astype(jnp.bfloat16)


def draw_key_rows(key, part):
    result = jnp.clip(jax.random.normal(jax.random.fold_in(key, 3), (TOKENS, H * HD), jnp.float32), -4.0, 4.0)
    return result.astype(jnp.bfloat16)


def draw_near_lists(key, part):
    device_count = NBLK // QB
    candidates = REACH * CAP
    picks_score = jax.random.randint(jax.random.fold_in(key, 21), (device_count, REACH, QB), 0, 1 << 20) * QB + jnp.arange(QB, dtype=jnp.int32)
    chosen = jnp.argsort(picks_score, axis=-1)[..., :CAP].astype(jnp.int32)
    device_ids = jnp.arange(device_count, dtype=jnp.int32)[:, None, None]
    hops = jnp.arange(1, REACH + 1, dtype=jnp.int32)[None, :, None]
    has_top = jnp.any(chosen == QB - 1, axis=-1, keepdims=True)
    first_slot = (jnp.arange(CAP, dtype=jnp.int32) == 0)[None, None, :]
    fixing = (device_ids == device_count - 1) & (hops == 1) & jnp.logical_not(has_top) & first_slot
    chosen = jnp.where(fixing, QB - 1, chosen).astype(jnp.int32)
    source = device_ids - hops
    listed = jnp.where(source >= 0, source * QB + chosen, -1).reshape(device_count, candidates)
    order_score = jax.random.randint(jax.random.fold_in(key, 22), (device_count, candidates), 0, 1 << 20) * candidates + jnp.arange(candidates, dtype=jnp.int32)
    order = jnp.argsort(order_score, axis=-1).astype(jnp.int32)
    slot_ids = ((jnp.arange(QB, dtype=jnp.int32)[:, None] * NEAR + jnp.arange(NEAR, dtype=jnp.int32)[None, :]) % candidates).reshape(-1)
    picked = jnp.take(order, slot_ids, axis=1)
    result = jnp.take_along_axis(listed, picked, axis=1)
    return result.reshape(device_count * QB, NEAR).astype(jnp.int32)


def touch_ends(values, key, least, high):
    shape = values.shape
    index_at = [jax.random.randint(jax.random.fold_in(key, axis), (), 0, shape[axis]) for axis in range(len(shape))]
    values = values.at[tuple(index_at)].set(least)
    longest = shape.index(max(shape))
    index_at[longest] = (index_at[longest] + 1) % shape[longest]
    return values.at[tuple(index_at)].set(high)


def block_scale(own_key, dims, pieces, least, high):
    gain, own = 1.0, jax.random.fold_in(own_key, 6)
    for position, shards_of in pieces:
        steps = jnp.exp(jax.random.uniform(jax.random.fold_in(own, position), (shards_of,), jnp.float32, least / len(pieces), high / len(pieces)))
        gain = gain * jnp.repeat(steps, dims[position] // shards_of).reshape([-1 if axis == position else 1 for axis in range(len(dims))])
    return gain


def normal_values(own_key, shape, scale, limit, split=(), kind=jnp.bfloat16):
    array = jax.random.normal(own_key, shape, jnp.float32) * scale
    if len(split) > 0:
        array = block_scale(own_key, shape, split, -0.22, 0.18) * array
    return jnp.clip(array, min=-limit, max=limit).astype(kind)


def setup_inputs(seed: int = 0, part: int = 0) -> dict:
    seeds = jax.random.split(jax.random.key(seed), 7)
    part_keys = jax.random.split(jax.random.fold_in(seeds[6], part), 7)
    queries = draw_queries(jax.random.fold_in(jax.random.fold_in(seeds[6], part), 71), part)
    key_rows = draw_key_rows(jax.random.fold_in(jax.random.fold_in(seeds[6], part), 71), part)
    value_rows = normal_values(part_keys[2], (TOKENS, H * HD), 1.0, 6.0, ((0, 16),))
    box_bins = touch_ends(jax.random.randint(part_keys[3], (2, TOKENS), 0, GRID), jax.random.fold_in(part_keys[3], 1), 0, GRID - 1).astype(jnp.int32)
    slopes = jnp.clip(jnp.exp(jax.random.uniform(seeds[4], (H,), jnp.float32, math.log(0.05), math.log(3.0))), 0.05, 3.0)
    near_lists = draw_near_lists(jax.random.fold_in(jax.random.fold_in(seeds[6], part), 71), part)
    return dict(queries=queries, key_rows=key_rows, value_rows=value_rows, box_bins=box_bins, slopes=slopes, near_lists=near_lists)


def attend(query_block, all_keys, all_values, query_bins, key_bins, present, slopes):
    row_count, features = query_block.shape
    head_count = slopes.shape[0]
    head_dim = features // head_count
    key_count = all_keys.shape[0]
    products = jnp.einsum('qhd,khd->hqk', query_block.astype(jnp.float32).reshape(row_count, head_count, head_dim), all_keys.astype(jnp.float32).reshape(key_count, head_count, head_dim))
    query_spot = query_bins.astype(jnp.float32)
    key_spot = key_bins.astype(jnp.float32)
    spread = jnp.abs(query_spot[0][:, None] - key_spot[0][None, :]) + jnp.abs(query_spot[1][:, None] - key_spot[1][None, :])
    scores = products * (1.0 / math.sqrt(head_dim)) - slopes[:, None, None] * (spread * 0.015625)[None]
    row_ids = jnp.arange(row_count, dtype=jnp.int32)[:, None]
    col_ids = jnp.arange(key_count, dtype=jnp.int32)[None, :]
    listed = jnp.concatenate([jnp.ones((row_count,), bool), jnp.repeat(present, row_count)])[None, :]
    allowed = jnp.where(col_ids < row_count, col_ids <= row_ids, listed)
    masked = jnp.where(allowed[None], scores, -jnp.inf)
    largest = lax.optimization_barrier(jnp.max(masked, axis=2, keepdims=True))
    exponent = jnp.exp(masked - largest)
    totals = lax.optimization_barrier(jnp.sum(exponent, axis=2))
    weights = lax.optimization_barrier(exponent.astype(jnp.bfloat16)).astype(jnp.float32)
    mixture = jnp.einsum('hqk,khd->qhd', weights, all_values.astype(jnp.float32).reshape(key_count, head_count, head_dim))
    return (mixture / jnp.transpose(totals)[:, :, None]).reshape(row_count, features).astype(jnp.bfloat16)

def reference(queries, key_rows, value_rows, box_bins, slopes, near_lists):
    features = queries.shape[1]
    query_blocks = queries.reshape(NBLK, BLOCK, features)
    key_blocks = key_rows.reshape(NBLK, BLOCK, features)
    value_blocks = value_rows.reshape(NBLK, BLOCK, features)
    all_bins = jnp.transpose(box_bins.reshape(2, NBLK, BLOCK), (1, 0, 2))

    def one_block(block_index):
        listed_ids = near_lists[block_index]
        present = listed_ids >= 0
        clamped = jnp.maximum(listed_ids, 0).astype(jnp.int32)
        all_keys = jnp.concatenate([key_blocks[block_index][None], jnp.take(key_blocks, clamped, axis=0)], 0).reshape(-1, features)
        all_values = jnp.concatenate([value_blocks[block_index][None], jnp.take(value_blocks, clamped, axis=0)], 0).reshape(-1, features)
        key_bins = jnp.concatenate([all_bins[block_index][None], jnp.take(all_bins, clamped, axis=0)], 0)
        key_bins = jnp.transpose(key_bins, (1, 0, 2)).reshape(2, -1)
        return attend(query_blocks[block_index], all_keys, all_values, all_bins[block_index], key_bins, present, slopes)
    results = lax.map(one_block, jnp.arange(NBLK, dtype=jnp.int32))
    return results.reshape(TOKENS, features)
```

```python
import functools
import math

import jax
import jax.numpy as jnp
from jax import lax
from jax.experimental import pallas as pl
from jax.experimental.pallas import tpu as pltpu
from jax.sharding import PartitionSpec as P

BLOCK = 128
REACH = 6
BLOCKS = 4
PIECES = 2 * BLOCKS
SPARE = 9 * BLOCKS
HIGH_ROAD = (0, 1)
LONG_ROAD = (0, 1, 2)


def exchange(n, k_ref, v_ref, bins_ref, wk_ref, wv_ref, wbins_ref, send_sems, recv_sems, bin_send, bin_recv, own_sems):
    me = lax.axis_index("seq")
    planes = n // 4
    a, b, c = me // 4, (me // 2) % 2, me % 2
    has_next, has_prev, has_prev2 = a < planes - 1, a >= 1, a >= 2
    up, across, beside = me + 4, me + 2 - 4 * b, me + 1 - 2 * c
    b0, b1, c0, c1 = b == 0, b == 1, c == 0, c == 1
    both = jnp.logical_and

    barrier = pltpu.get_barrier_semaphore()
    for d in range(1, REACH + 1):

        @pl.when(me >= d)
        def _():
            pl.semaphore_signal(barrier, inc=1, device_id={"seq": me - d}, device_id_type=pl.DeviceIdType.MESH)

        @pl.when(me + d < n)
        def _():
            pl.semaphore_signal(barrier, inc=1, device_id={"seq": me + d}, device_id_type=pl.DeviceIdType.MESH)

    pl.semaphore_wait(barrier, jnp.minimum(me, REACH) + jnp.minimum(n - 1 - me, REACH))

    def own(t):
        return (k_ref, v_ref)[t // BLOCKS].at[t % BLOCKS]

    def slot(index, t):
        return (wk_ref, wv_ref)[t // BLOCKS].at[index * BLOCKS + t % BLOCKS]

    sent = []

    def send(flow, t, source, index, target, cond):
        def copy():
            return pltpu.make_async_remote_copy(
                src_ref=own(t) if source is None else slot(source, t),
                dst_ref=slot(index, t),
                send_sem=send_sems.at[flow, t],
                recv_sem=recv_sems.at[index, t],
                device_id={"seq": target},
                device_id_type=pl.DeviceIdType.MESH,
            )

        @pl.when(cond)
        def _():
            copy().start()

        sent.append((copy, cond))

    def arrive(index, t, cond):
        @pl.when(cond)
        def _():
            pltpu.make_async_remote_copy(
                src_ref=slot(index, t),
                dst_ref=slot(index, t),
                send_sem=send_sems.at[0, t],
                recv_sem=recv_sems.at[index, t],
                device_id={"seq": beside},
                device_id_type=pl.DeviceIdType.MESH,
            ).wait_recv()

    def bin_copy(d, device):
        return pltpu.make_async_remote_copy(
            src_ref=bins_ref,
            dst_ref=wbins_ref.at[d - 1],
            send_sem=bin_send.at[d - 1],
            recv_sem=bin_recv.at[d - 1],
            device_id={"seq": device},
            device_id_type=pl.DeviceIdType.MESH,
        )

    for d in range(1, REACH + 1):

        @pl.when(me + d < n)
        def _():
            bin_copy(d, me + d).start()

    for t in range(PIECES):
        send(0, t, None, 3 + 2 * b + c, up, has_next)
        send(1, t, None, c, across, b0)
        send(2, t, None, 2 * b, beside, c0)
    spares = [
        pltpu.make_async_copy(own(0), wk_ref.at[SPARE], own_sems.at[0]),
        pltpu.make_async_copy(own(BLOCKS), wv_ref.at[SPARE], own_sems.at[1]),
    ]
    for spare in spares:
        spare.start()

    two_up = both(has_prev, has_next)
    for t in range(PIECES):
        arrive(3 + 2 * b + c, t, has_prev)
        send(3, t, 3 + 2 * b + c, 3 + 2 * b + c, beside, has_prev)
        if t in LONG_ROAD:
            send(4, t, 3 + 2 * b + c, 3 + 2 * b + c, across, both(has_prev, b1))
        else:
            send(4, t, 3 + 2 * b + c, 3 + 2 * b + c, across, has_prev)
        if t in HIGH_ROAD:
            send(5, t, 5 + c, 7 + c, up, both(two_up, b1))
        arrive(c, t, b1)
        send(6, t, c, c, beside, b1)
        if t in LONG_ROAD:
            send(7, t, c, 3 + c, up, both(has_next, b1))
        arrive(5 + c, t, both(has_prev, b0))
        send(6, t, 5 + c, 5 + c, beside, both(has_prev, b0))
        if t not in HIGH_ROAD:
            send(5, t, 5 + c, 7 + c, up, both(two_up, b0))
    for t in HIGH_ROAD:
        arrive(7 + c, t, both(has_prev2, b1))
        send(8, t, 7 + c, 7 + c, across, both(has_prev2, b1))
    for t in list(LONG_ROAD) + [t for t in range(PIECES) if t not in LONG_ROAD]:
        arrive(3 + c, t, both(has_prev, b1))
        send(9, t, 3 + c, 3 + c, beside, both(has_prev, both(b1, c1)))
    for t in [t for t in range(PIECES) if t not in HIGH_ROAD] + list(HIGH_ROAD):
        arrive(7 + c, t, both(has_prev2, b0))
        send(9, t, 7 + c, 7 + c, beside, both(has_prev2, both(b0, c1)))

    for t in range(PIECES):
        arrive(2 * b, t, c1)
        arrive(4 + 2 * b - c, t, has_prev)
        arrive(1 - c, t, b1)
        arrive(6 - c, t, both(has_prev, b0))
        arrive(4, t, both(has_prev, both(b1, c0)))
        arrive(8, t, both(has_prev2, both(b0, c0)))
    for d in range(1, REACH + 1):

        @pl.when(me >= d)
        def _():
            bin_copy(d, me).wait_recv()

    for copy, cond in sent:

        @pl.when(cond)
        def _(copy=copy):
            copy().wait_send()

    for d in range(1, REACH + 1):

        @pl.when(me + d < n)
        def _():
            bin_copy(d, me + d).wait_send()

    for spare in spares:
        spare.wait()


def attend(near, heads, places_ref, bin_places_ref, slopes_ref, q_ref, k_ref, v_ref, bins_ref, wbins_ref, *rest):
    key_refs = (k_ref,) + rest[:near]
    value_refs = (v_ref,) + rest[near : 2 * near]
    out_ref, bias = rest[2 * near :]
    block = pl.program_id(0)
    own = bins_ref[block].astype(jnp.float32)
    rows_x = jnp.transpose(jnp.broadcast_to(own[0:1], (BLOCK, BLOCK)))
    rows_y = jnp.transpose(jnp.broadcast_to(own[1:2], (BLOCK, BLOCK)))
    row_ids = lax.broadcasted_iota(jnp.int32, (BLOCK, BLOCK), 0)
    col_ids = lax.broadcasted_iota(jnp.int32, (BLOCK, BLOCK), 1)
    for j in range(near + 1):
        if j == 0:
            spots, allowed = own, col_ids <= row_ids
        else:
            place = bin_places_ref[block, j - 1]
            spots = wbins_ref[jnp.maximum(place, 0)].astype(jnp.float32)
            allowed = (col_ids * 0 + place) >= 0
        spread = jnp.abs(rows_x - spots[0:1]) + jnp.abs(rows_y - spots[1:2])
        bias[:, j * BLOCK : (j + 1) * BLOCK] = jnp.where(allowed, spread * 0.015625, jnp.inf)
    dim = q_ref.shape[-1] // heads
    factor = math.log2(math.e)
    for h in range(heads):
        cols = slice(h * dim, (h + 1) * dim)
        query = q_ref[0, :, cols]
        keys = jnp.concatenate([ref[0, :, cols] for ref in key_refs], 0)
        values = jnp.concatenate([ref[0, :, cols] for ref in value_refs], 0)
        products = lax.dot_general(query, keys, (((1,), (1,)), ((), ())), preferred_element_type=jnp.float32)
        scores = products * (factor / math.sqrt(dim)) - (slopes_ref[h] * factor) * bias[...]
        largest = jnp.max(scores, axis=1, keepdims=True)
        exponent = jnp.exp2(scores - largest)
        totals = jnp.sum(exponent, axis=1, keepdims=True)
        mixture = jnp.dot(exponent.astype(jnp.bfloat16), values, preferred_element_type=jnp.float32)
        out_ref[0, :, cols] = (mixture / totals).astype(jnp.bfloat16)


def body(n, queries, key_rows, value_rows, box_bins, slopes, near_lists):
    token_count, features = queries.shape
    blocks = token_count // BLOCK
    near = near_lists.shape[1]
    heads = slopes.shape[0]
    device = lax.axis_index("seq")
    shape = (blocks, BLOCK, features)
    queries, key_rows, value_rows = (x.reshape(shape) for x in (queries, key_rows, value_rows))
    bins = jnp.transpose(box_bins.reshape(2, blocks, BLOCK), (1, 0, 2))
    lists = lax.dynamic_slice_in_dim(near_lists, device * blocks, blocks, 0)
    source, inside = lists // blocks, lists % blocks
    index = source % 4 + jnp.array([0, 3, 5], jnp.int32)[jnp.clip(device // 4 - source // 4, 0, 2)]
    places = jnp.where(lists >= 0, index * blocks + inside, SPARE)
    bin_places = jnp.where(lists >= 0, (device - source - 1) * blocks + inside, -1)

    anywhere = pl.BlockSpec(memory_space=pl.ANY)
    wk, wv, wbins = pl.pallas_call(
        functools.partial(exchange, n),
        out_shape=(
            jax.ShapeDtypeStruct((SPARE + 1, BLOCK, features), key_rows.dtype),
            jax.ShapeDtypeStruct((SPARE + 1, BLOCK, features), value_rows.dtype),
            jax.ShapeDtypeStruct((REACH, blocks, 2, BLOCK), jnp.int32),
        ),
        in_specs=[anywhere] * 3,
        out_specs=(anywhere,) * 3,
        scratch_shapes=[
            pltpu.SemaphoreType.DMA((10, PIECES)),
            pltpu.SemaphoreType.DMA((9, PIECES)),
            pltpu.SemaphoreType.DMA((REACH,)),
            pltpu.SemaphoreType.DMA((REACH,)),
            pltpu.SemaphoreType.DMA((2,)),
        ],
        compiler_params=pltpu.CompilerParams(collective_id=0, has_side_effects=True),
        name="exchange",
    )(key_rows, value_rows, bins)

    tile = (1, BLOCK, features)
    mine = pl.BlockSpec(tile, lambda i, *_: (i, 0, 0))
    listed = [pl.BlockSpec(tile, lambda i, places, *_, j=j: (places[i, j], 0, 0)) for j in range(near)]
    whole = pl.BlockSpec(memory_space=pltpu.VMEM)
    out = pl.pallas_call(
        functools.partial(attend, near, heads),
        grid_spec=pltpu.PrefetchScalarGridSpec(
            num_scalar_prefetch=3,
            grid=(blocks,),
            in_specs=[mine, mine, mine, whole, whole] + listed + listed,
            out_specs=mine,
            scratch_shapes=[pltpu.VMEM((BLOCK, (near + 1) * BLOCK), jnp.float32)],
        ),
        out_shape=jax.ShapeDtypeStruct(shape, jnp.bfloat16),
        compiler_params=pltpu.CompilerParams(vmem_limit_bytes=48 << 20),
        name="attend",
    )(places, bin_places, slopes, queries, key_rows, value_rows, bins, wbins.reshape(REACH * blocks, 2, BLOCK), *([wk] * near), *([wv] * near))
    return out.reshape(token_count, features)


def solution(mesh):
    placed = (
        P(("grp", "seq"), None),
        P(("grp", "seq"), None),
        P(("grp", "seq"), None),
        P(None, ("grp", "seq")),
        P(),
        P("grp", None),
    )
    return jax.shard_map(
        functools.partial(body, mesh.shape["seq"]),
        mesh=mesh,
        in_specs=placed,
        out_specs=P(("grp", "seq"), None),
        check_vma=False,
    )
```

```python
import functools
import math

import jax
import jax.numpy as jnp
from jax import lax
from jax.experimental import pallas as pl
from jax.experimental.pallas import tpu as pltpu
from jax.sharding import PartitionSpec as P

BLOCK = 128
REACH = 6
BLOCKS = 4
PIECES = 2 * BLOCKS
SPARE = 9 * BLOCKS
HIGH_ROAD = (0, 1)
ORDER = (0, 1, 4, 5, 2, 3, 6, 7)
LONG_ROAD = (0, 1)


def exchange(n, k_ref, v_ref, bins_ref, wk_ref, wv_ref, wbins_ref, send_sems, recv_sems, bin_send, bin_recv, own_sems):
    me = lax.axis_index("seq")
    planes = n // 4
    a, b, c = me // 4, (me // 2) % 2, me % 2
    has_next, has_prev, has_prev2 = a < planes - 1, a >= 1, a >= 2
    up, across, beside = me + 4, me + 2 - 4 * b, me + 1 - 2 * c
    b0, b1, c0, c1 = b == 0, b == 1, c == 0, c == 1
    both = jnp.logical_and

    def kept(t, cond):
        return cond if t % BLOCKS < 2 else both(cond, c1)


    barrier = pltpu.get_barrier_semaphore()
    for d in range(1, REACH + 1):

        @pl.when(me >= d)
        def _():
            pl.semaphore_signal(barrier, inc=1, device_id={"seq": me - d}, device_id_type=pl.DeviceIdType.MESH)

        @pl.when(me + d < n)
        def _():
            pl.semaphore_signal(barrier, inc=1, device_id={"seq": me + d}, device_id_type=pl.DeviceIdType.MESH)

    pl.semaphore_wait(barrier, jnp.minimum(me, REACH) + jnp.minimum(n - 1 - me, REACH))

    def own(t):
        return (k_ref, v_ref)[t // BLOCKS].at[t % BLOCKS]

    def slot(index, t):
        return (wk_ref, wv_ref)[t // BLOCKS].at[index * BLOCKS + t % BLOCKS]

    sent = []

    def send(flow, t, source, index, target, cond):
        def copy():
            return pltpu.make_async_remote_copy(
                src_ref=own(t) if source is None else slot(source, t),
                dst_ref=slot(index, t),
                send_sem=send_sems.at[flow, t],
                recv_sem=recv_sems.at[index, t],
                device_id={"seq": target},
                device_id_type=pl.DeviceIdType.MESH,
            )

        @pl.when(cond)
        def _():
            copy().start()

        sent.append((copy, cond))

    def arrive(index, t, cond):
        @pl.when(cond)
        def _():
            pltpu.make_async_remote_copy(
                src_ref=slot(index, t),
                dst_ref=slot(index, t),
                send_sem=send_sems.at[0, t],
                recv_sem=recv_sems.at[index, t],
                device_id={"seq": beside},
                device_id_type=pl.DeviceIdType.MESH,
            ).wait_recv()

    def bin_copy(d, device):
        return pltpu.make_async_remote_copy(
            src_ref=bins_ref,
            dst_ref=wbins_ref.at[d - 1],
            send_sem=bin_send.at[d - 1],
            recv_sem=bin_recv.at[d - 1],
            device_id={"seq": device},
            device_id_type=pl.DeviceIdType.MESH,
        )

    for d in range(1, REACH + 1):

        @pl.when(me + d < n)
        def _():
            bin_copy(d, me + d).start()

    for t in ORDER:
        send(0, t, None, 3 + 2 * b + c, up, has_next)
        send(1, t, None, c, across, b0)
        send(2, t, None, 2 * b, beside, c0)
    spares = [
        pltpu.make_async_copy(own(0), wk_ref.at[SPARE], own_sems.at[0]),
        pltpu.make_async_copy(own(BLOCKS), wv_ref.at[SPARE], own_sems.at[1]),
    ]
    for spare in spares:
        spare.start()

    two_up = both(has_prev, has_next)
    for t in ORDER:
        arrive(3 + 2 * b + c, t, has_prev)
        send(3, t, 3 + 2 * b + c, 3 + 2 * b + c, beside, has_prev)
        if t in LONG_ROAD:
            send(4, t, 3 + 2 * b + c, 3 + 2 * b + c, across, both(has_prev, b1))
        else:
            send(4, t, 3 + 2 * b + c, 3 + 2 * b + c, across, both(has_prev, jnp.logical_or(b1, kept(t, b0))))
        if t in HIGH_ROAD:
            send(5, t, 5 + c, 7 + c, up, both(two_up, b1))
        arrive(c, t, b1)
        send(6, t, c, c, beside, b1)
        if t in LONG_ROAD:
            send(7, t, c, 3 + c, up, both(has_next, b1))
        arrive(5 + c, t, both(has_prev, b0))
        send(6, t, 5 + c, 5 + c, beside, both(has_prev, b0))
        if t not in HIGH_ROAD:
            send(5, t, 5 + c, 7 + c, up, kept(t, both(two_up, b0)))
    for t in HIGH_ROAD:
        arrive(7 + c, t, both(has_prev2, b1))
        send(8, t, 7 + c, 7 + c, across, both(has_prev2, b1))
    for t in ORDER:
        arrive(3 + c, t, kept(t, both(has_prev, b1)))
        send(9, t, 3 + c, 3 + c, beside, both(has_prev, both(b1, c1)))
    for t in [t for t in ORDER if t not in HIGH_ROAD] + list(HIGH_ROAD):
        arrive(7 + c, t, kept(t, both(has_prev2, b0)))
        send(9, t, 7 + c, 7 + c, beside, both(has_prev2, both(b0, c1)))

    for t in ORDER:
        arrive(2 * b, t, c1)
        arrive(4 + 2 * b - c, t, has_prev)
        arrive(1 - c, t, b1)
        arrive(6 - c, t, both(has_prev, b0))
        arrive(4, t, both(has_prev, both(b1, c0)))
        arrive(8, t, both(has_prev2, both(b0, c0)))
    for d in range(1, REACH + 1):

        @pl.when(me >= d)
        def _():
            bin_copy(d, me).wait_recv()

    for copy, cond in sent:

        @pl.when(cond)
        def _(copy=copy):
            copy().wait_send()

    for d in range(1, REACH + 1):

        @pl.when(me + d < n)
        def _():
            bin_copy(d, me + d).wait_send()

    for spare in spares:
        spare.wait()


def reorder(places_ref, k_ref, v_ref, k_out, v_out):
    k_out[...] = k_ref[...]
    v_out[...] = v_ref[...]


def attend(near, heads, places_ref, bin_places_ref, slopes_ref, q_ref, k_ref, v_ref, bins_ref, wbins_ref, *rest):
    key_refs = (k_ref,) + rest[:near]
    value_refs = (v_ref,) + rest[near : 2 * near]
    out_ref, bias = rest[2 * near :]
    block = pl.program_id(0)
    own = bins_ref[block].astype(jnp.float32)
    rows_x = jnp.transpose(jnp.broadcast_to(own[0:1], (BLOCK, BLOCK)))
    rows_y = jnp.transpose(jnp.broadcast_to(own[1:2], (BLOCK, BLOCK)))
    row_ids = lax.broadcasted_iota(jnp.int32, (BLOCK, BLOCK), 0)
    col_ids = lax.broadcasted_iota(jnp.int32, (BLOCK, BLOCK), 1)
    for j in range(near + 1):
        if j == 0:
            spots, allowed = own, col_ids <= row_ids
        else:
            place = bin_places_ref[block, j - 1]
            spots = wbins_ref[jnp.maximum(place, 0)].astype(jnp.float32)
            allowed = (col_ids * 0 + place) >= 0
        spread = jnp.abs(rows_x - spots[0:1]) + jnp.abs(rows_y - spots[1:2])
        bias[:, j * BLOCK : (j + 1) * BLOCK] = jnp.where(allowed, spread * 0.015625, jnp.inf)
    dim = q_ref.shape[-1] // heads
    factor = math.log2(math.e)
    for h in range(heads):
        cols = slice(h * dim, (h + 1) * dim)
        query = q_ref[0, :, cols]
        keys = jnp.concatenate([ref[0, :, cols] for ref in key_refs], 0)
        values = jnp.concatenate([ref[0, :, cols] for ref in value_refs], 0)
        products = lax.dot_general(query, keys, (((1,), (1,)), ((), ())), preferred_element_type=jnp.float32)
        scores = products * (factor / math.sqrt(dim)) - (slopes_ref[h] * factor) * bias[...]
        largest = jnp.max(scores, axis=1, keepdims=True)
        exponent = jnp.exp2(scores - largest)
        totals = jnp.sum(exponent, axis=1, keepdims=True)
        mixture = jnp.dot(exponent.astype(jnp.bfloat16), values, preferred_element_type=jnp.float32)
        out_ref[0, :, cols] = (mixture / totals).astype(jnp.bfloat16)


def body(n, queries, key_rows, value_rows, box_bins, slopes, near_lists):
    token_count, features = queries.shape
    blocks = token_count // BLOCK
    near = near_lists.shape[1]
    heads = slopes.shape[0]
    device = lax.axis_index("seq")
    shape = (blocks, BLOCK, features)
    queries, key_rows, value_rows = (x.reshape(shape) for x in (queries, key_rows, value_rows))
    bins = jnp.transpose(box_bins.reshape(2, blocks, BLOCK), (1, 0, 2))
    lists = lax.dynamic_slice_in_dim(near_lists, device * blocks, blocks, 0)
    source, inside = lists // blocks, lists % blocks
    index = source % 4 + jnp.array([0, 3, 5], jnp.int32)[jnp.clip(device // 4 - source // 4, 0, 2)]
    block_ids = jnp.arange(n * blocks, dtype=jnp.int32).reshape(n, blocks)
    far_lists = jnp.pad(near_lists.reshape(n, -1), ((0, REACH), (0, 0)), constant_values=-1)[REACH:]
    first = jnp.any(far_lists[:, None, :] == block_ids[:, :, None], axis=2)
    ahead = jnp.logical_or(
        jnp.logical_and(first[:, None, :], jnp.logical_not(first)[:, :, None]),
        jnp.logical_and(first[:, None, :] == first[:, :, None], jnp.tri(blocks, k=-1, dtype=bool)[None]),
    )
    order = jnp.sum(ahead.astype(jnp.int32), axis=2)
    same = jnp.maximum(lists, 0)[:, :, None] == block_ids.reshape(-1)
    inside_sent = jnp.sum(jnp.where(same, order.reshape(-1), 0), axis=2)
    places = jnp.where(lists >= 0, index * blocks + inside_sent, SPARE)
    own_order = lax.dynamic_slice_in_dim(order, device, 1, 0)[0]
    bin_places = jnp.where(lists >= 0, (device - source - 1) * blocks + inside, -1)

    tile = (1, BLOCK, features)
    mine = pl.BlockSpec(tile, lambda i, *_: (i, 0, 0))
    moved = pl.BlockSpec(tile, lambda i, places: (places[i], 0, 0))
    sent_keys, sent_values = pl.pallas_call(
        reorder,
        grid_spec=pltpu.PrefetchScalarGridSpec(
            num_scalar_prefetch=1, grid=(blocks,), in_specs=[mine, mine], out_specs=(moved, moved)
        ),
        out_shape=(jax.ShapeDtypeStruct(shape, key_rows.dtype), jax.ShapeDtypeStruct(shape, value_rows.dtype)),
        name="reorder",
    )(own_order, key_rows, value_rows)

    anywhere = pl.BlockSpec(memory_space=pl.ANY)
    wk, wv, wbins = pl.pallas_call(
        functools.partial(exchange, n),
        out_shape=(
            jax.ShapeDtypeStruct((SPARE + 1, BLOCK, features), key_rows.dtype),
            jax.ShapeDtypeStruct((SPARE + 1, BLOCK, features), value_rows.dtype),
            jax.ShapeDtypeStruct((REACH, blocks, 2, BLOCK), jnp.int32),
        ),
        in_specs=[anywhere] * 3,
        out_specs=(anywhere,) * 3,
        scratch_shapes=[
            pltpu.SemaphoreType.DMA((10, PIECES)),
            pltpu.SemaphoreType.DMA((9, PIECES)),
            pltpu.SemaphoreType.DMA((REACH,)),
            pltpu.SemaphoreType.DMA((REACH,)),
            pltpu.SemaphoreType.DMA((2,)),
        ],
        compiler_params=pltpu.CompilerParams(collective_id=0, has_side_effects=True),
        name="exchange",
    )(sent_keys, sent_values, bins)

    listed = [pl.BlockSpec(tile, lambda i, places, *_, j=j: (places[i, j], 0, 0)) for j in range(near)]
    whole = pl.BlockSpec(memory_space=pltpu.VMEM)
    out = pl.pallas_call(
        functools.partial(attend, near, heads),
        grid_spec=pltpu.PrefetchScalarGridSpec(
            num_scalar_prefetch=3,
            grid=(blocks,),
            in_specs=[mine, mine, mine, whole, whole] + listed + listed,
            out_specs=mine,
            scratch_shapes=[pltpu.VMEM((BLOCK, (near + 1) * BLOCK), jnp.float32)],
        ),
        out_shape=jax.ShapeDtypeStruct(shape, jnp.bfloat16),
        compiler_params=pltpu.CompilerParams(vmem_limit_bytes=48 << 20),
        name="attend",
    )(places, bin_places, slopes, queries, key_rows, value_rows, bins, wbins.reshape(REACH * blocks, 2, BLOCK), *([wk] * near), *([wv] * near))
    return out.reshape(token_count, features)


def solution(mesh):
    placed = (
        P(("grp", "seq"), None),
        P(("grp", "seq"), None),
        P(("grp", "seq"), None),
        P(None, ("grp", "seq")),
        P(),
        P("grp", None),
    )
    return jax.shard_map(
        functools.partial(body, mesh.shape["seq"]),
        mesh=mesh,
        in_specs=placed,
        out_specs=P(("grp", "seq"), None),
        check_vma=False,
    )
```
